256 devices in a mesh: st: 128 (over z, x_lo, y, core), row: 2 (over x_hi).
Axes of the slice: x: 4 (x_hi: 2, x_lo: 2; x = x_hi * 2 + x_lo), y: 4, z: 8, core: 2. Of those that a mesh axis runs over, the one named last changes fastest.
Arguments:
- forcing: bfloat16 [2, 128, 1024, 256], P(None, 'st', 'row'), may hold values from -6 to 6
- inverse_first: bfloat16 [2, 128, 1024, 1024], P(None, 'st', 'row'), may hold values from -0.1875 to 0.1875
- lower_first: bfloat16 [2, 128, 1024, 1024], P(None, 'st', 'row'), may hold values from -0.1875 to 0.1875
- upper_first: bfloat16 [2, 128, 1024, 1024], P(None, 'st', 'row'), may hold values from -0.1875 to 0.1875
- inverse_second: bfloat16 [2, 128, 1024, 1024], P(None, 'st', 'row'), may hold values from -0.1875 to 0.1875
- lower_second: bfloat16 [2, 128, 1024, 1024], P(None, 'st', 'row'), may hold values from -0.1875 to 0.1875
- upper_second: bfloat16 [2, 128, 1024, 1024], P(None, 'st', 'row'), may hold values from -0.1875 to 0.1875
Outputs:
- reduced_forcing: bfloat16 [2, 128, 1024, 256], P(None, 'st', 'row')
The draws below stay inside these ranges and needn't reach their ends.
All inputs are finite; a program needn't handle non-finite values.
Results may differ from the reference program's by a relative error of at most 0.0059.
Values may be sent and summed in bfloat16 or wider, within the bound.
No kernel may reach another device: no remote copies, remote signals or barrier semaphores. Data moves between devices by JAX's collectives and lax.ppermute only.
A program may use at most 64 MiB of HBM per device.

```python
import jax
import jax.numpy as jnp
from jax import lax

M = 1024
R = 256
STN_DEV = 2
STATIONS = 256


def levels(key, shape, pieces, least, top_value):
    def one(axis_at, blocks):
        heights = jax.random.uniform(jax.random.fold_in(jax.random.fold_in(key, 6), axis_at), (blocks,), jnp.float32, least / len(pieces), top_value / len(pieces))
        return jnp.repeat(jnp.exp(heights), shape[axis_at] // blocks).reshape((-1,) + (1,) * (len(shape) - axis_at - 1))

    level = one(*pieces[0])
    for cut in pieces[1:]:
        level = level * one(*cut)
    return level


def scatter_about(own_key, shape, scale, most, shards=(), dtype=jnp.bfloat16):
    values = jax.random.normal(own_key, shape, jnp.float32) * scale
    if len(shards) > 0:
        values = levels(own_key, shape, shards, -0.22, 0.18) * values
    return jnp.clip(values, min=-most, max=most).astype(dtype)


def setup_inputs(seed: int = 0) -> dict:
    streams_of = jax.random.split(jax.random.key(seed), 8)
    forcing = scatter_about(streams_of[0], (STN_DEV, STATIONS // STN_DEV, M, R), 1.0, 6.0, ((1, 128), (2, 2)))
    inverse_first = scatter_about(streams_of[1], (STN_DEV, STATIONS // STN_DEV, M, M), M ** -0.5, 0.1875, ((1, 128), (2, 2)))
    lower_first = scatter_about(streams_of[2], (STN_DEV, STATIONS // STN_DEV, M, M), M ** -0.5, 0.1875, ((1, 128), (2, 2)))
    upper_first = scatter_about(streams_of[3], (STN_DEV, STATIONS // STN_DEV, M, M), M ** -0.5, 0.1875, ((1, 128), (2, 2)))
    inverse_second = scatter_about(streams_of[4], (STN_DEV, STATIONS // STN_DEV, M, M), M ** -0.5, 0.1875, ((1, 128), (2, 2)))
    lower_second = scatter_about(streams_of[5], (STN_DEV, STATIONS // STN_DEV, M, M), M ** -0.5, 0.1875, ((1, 128), (2, 2)))
    upper_second = scatter_about(streams_of[6], (STN_DEV, STATIONS // STN_DEV, M, M), M ** -0.5, 0.1875, ((1, 128), (2, 2)))
    return dict(forcing=forcing, inverse_first=inverse_first, lower_first=lower_first, upper_first=upper_first, inverse_second=inverse_second, lower_second=lower_second, upper_second=upper_second)


def pair_dot(blocks):
    return jnp.dot(blocks[0], blocks[1], preferred_element_type=jnp.float32)


def two_dots(blocks):
    first = jnp.dot(blocks[0], blocks[1], preferred_element_type=jnp.float32)
    return first + jnp.dot(blocks[2], blocks[3], preferred_element_type=jnp.float32)


def reduce_level(forcing_now, inverse, lower, upper, stride):
    scaled = lax.map(pair_dot, (inverse, forcing_now)).astype(jnp.bfloat16)
    zero_rows = jnp.zeros((stride,) + scaled.shape[1:], jnp.bfloat16)
    from_below = jnp.concatenate([zero_rows, scaled[:-stride]], axis=0)
    from_above = jnp.concatenate([scaled[stride:], zero_rows], axis=0)
    coupled = lax.map(two_dots, (lower, from_below, upper, from_above))
    return (forcing_now.astype(jnp.float32) - coupled).astype(jnp.bfloat16)


def reference(forcing, inverse_first, lower_first, upper_first, inverse_second, lower_second, upper_second):
    station_count = forcing.shape[0] * forcing.shape[1]

    def flatten(array):
        return array.reshape((station_count,) + array.shape[2:])

    forcing_first = reduce_level(flatten(forcing), flatten(inverse_first), flatten(lower_first), flatten(upper_first), 1)
    reduced = reduce_level(forcing_first, flatten(inverse_second), flatten(lower_second), flatten(upper_second), 2)
    return reduced.reshape(forcing.shape)
```

```python
import jax
import jax.numpy as jnp
from jax import lax
from jax.experimental import pallas as pl
from jax.experimental.pallas import tpu as pltpu
from jax.sharding import PartitionSpec as P

CHUNKS = 2


def shift(value, steps):
    count = lax.axis_size("st")
    pairs = [(source, (source + steps) % count) for source in range(count)]
    return lax.ppermute(value, "st", pairs)


def swap(value):
    return lax.ppermute(value, "row", [(0, 1), (1, 0)])


def dot(a, b):
    return jnp.dot(a, b, preferred_element_type=jnp.float32)


def scale_kernel(where_ref, own_cols, other_cols, own, other, out):
    del where_ref
    total = dot(own_cols[...], own[...]) + dot(other_cols[...], other[...])
    out[...] = total.astype(out.dtype)


def scale(where, inverse, own, own_spec, other):
    stations, _, rows, wide = inverse.shape
    columns = other.shape[-1]
    half = wide // 2
    return pl.pallas_call(
        scale_kernel,
        out_shape=jax.ShapeDtypeStruct((stations, rows, columns), jnp.bfloat16),
        grid_spec=pltpu.PrefetchScalarGridSpec(
            num_scalar_prefetch=1,
            grid=(stations,),
            in_specs=[
                pl.BlockSpec((None, None, rows, half), lambda j, w: (j, 0, 0, w[0])),
                pl.BlockSpec((None, None, rows, half), lambda j, w: (j, 0, 0, 1 - w[0])),
                own_spec,
                pl.BlockSpec((None, rows, columns), lambda j, w: (j, 0, 0)),
            ],
            out_specs=pl.BlockSpec((None, rows, columns), lambda j, w: (j, 0, 0)),
        ),
        compiler_params=pltpu.CompilerParams(vmem_limit_bytes=16 * 2**20),
        cost_estimate=pl.CostEstimate(
            flops=2 * stations * rows * wide * columns,
            bytes_accessed=2 * stations * rows * (wide + 3 * columns),
            transcendentals=0,
        ),
        name="scale",
    )(where, inverse, inverse, own, other)


def couple_kernel(where_ref, lo_a, lo_b, up_a, up_b, below_a, below_b, above_a, above_b, now, *rest):
    out = rest[-1]
    j = pl.program_id(0)
    below = dot(lo_a[...], below_a[...]) + dot(lo_b[...], below_b[...])
    above = dot(up_a[...], above_a[...]) + dot(up_b[...], above_b[...])
    has_below = (j > 0) | (where_ref[1] == 0)
    has_above = (j < pl.num_programs(0) - 1) | (where_ref[2] == 0)
    coupled = jnp.where(has_below, below, 0.0) + jnp.where(has_above, above, 0.0)
    out[...] = (now[...].astype(jnp.float32) - coupled).astype(out.dtype)


def couple(where, lower, upper, below, above, now, now_spec, out_shape, out_spec, into=None):
    stations, _, rows, wide = lower.shape
    columns = below[0].shape[-1]
    half = wide // 2
    last = stations - 1

    def block(own):
        if own:
            return pl.BlockSpec((None, None, rows, half), lambda j, w: (j, 0, 0, w[0]))
        return pl.BlockSpec((None, None, rows, half), lambda j, w: (j, 0, 0, 1 - w[0]))

    def from_below():
        return pl.BlockSpec((None, rows, columns), lambda j, w: (jnp.maximum(j - w[1], 0), 0, 0))

    def from_above():
        return pl.BlockSpec((None, rows, columns), lambda j, w: (jnp.minimum(j + w[2], last), 0, 0))

    operands = [where, lower, lower, upper, upper, *below, *above, now]
    in_specs = [block(True), block(False), block(True), block(False)]
    in_specs += [from_below(), from_below(), from_above(), from_above(), now_spec]
    aliases = {}
    if into is not None:
        aliases = {len(operands): 0}
        operands.append(into)
        in_specs.append(pl.BlockSpec(memory_space=pl.ANY))
    return pl.pallas_call(
        couple_kernel,
        out_shape=out_shape,
        grid_spec=pltpu.PrefetchScalarGridSpec(
            num_scalar_prefetch=1, grid=(stations,), in_specs=in_specs, out_specs=out_spec
        ),
        input_output_aliases=aliases,
        compiler_params=pltpu.CompilerParams(vmem_limit_bytes=24 * 2**20),
        cost_estimate=pl.CostEstimate(
            flops=4 * stations * rows * wide * columns,
            bytes_accessed=2 * stations * rows * (2 * wide + 6 * columns),
            transcendentals=0,
        ),
        name="couple",
    )(*operands)


def on_device(forcing, inv1, low1, up1, inv2, low2, up2):
    stations, _, rows, columns = forcing.shape
    piece = columns // CHUNKS
    row = lax.axis_index("row")
    position = lax.axis_index("st")
    count = lax.axis_size("st")

    def where(stride):
        wraps = [position < stride, position >= count - stride]
        return jnp.stack([row] + [flag.astype(jnp.int32) for flag in wraps])

    where1, where2 = where(1), where(2)

    def wide_spec(c):
        return pl.BlockSpec((None, None, rows, piece), lambda j, w: (j, 0, 0, c))

    def slim_spec():
        return pl.BlockSpec((None, rows, piece), lambda j, w: (j, 0, 0))

    slim = jax.ShapeDtypeStruct((stations, rows, piece), jnp.bfloat16)

    def neighbours(scaled, stride):
        below_own, above_own = shift(scaled, stride), shift(scaled, -stride)
        other = swap(scaled)
        return (below_own, shift(other, stride)), (above_own, shift(other, -stride))

    out = None
    for c in range(CHUNKS):
        mine = forcing[:, 0, :, c * piece : (c + 1) * piece]
        scaled = scale(where1, inv1, forcing, wide_spec(c), swap(mine))
        below, above = neighbours(scaled, 1)
        first = couple(
            where1, low1, up1, below, above, forcing, wide_spec(c), slim, slim_spec()
        )
        scaled = scale(where2, inv2, first, slim_spec(), swap(first))
        below, above = neighbours(scaled, 2)
        out = couple(
            where2, low2, up2, below, above, first, slim_spec(),
            jax.ShapeDtypeStruct(forcing.shape, forcing.dtype), wide_spec(c), out,
        )
    return out


def solution(mesh):
    spec = P(None, "st", "row", None)
    return jax.shard_map(
        on_device, mesh=mesh, in_specs=(spec,) * 7, out_specs=spec, check_vma=False
    )
```

```python
import jax
import jax.numpy as jnp
from jax import lax
from jax.experimental import pallas as pl
from jax.experimental.pallas import tpu as pltpu
from jax.sharding import PartitionSpec as P

CHUNKS = 2


def shift(value, steps):
    count = lax.axis_size("st")
    pairs = [(source, (source + steps) % count) for source in range(count)]
    return lax.ppermute(value, "st", pairs)


def shift_across(value, steps):
    count = lax.axis_size("st")
    pairs = [
        (2 * source + row, 2 * ((source + steps) % count) + 1 - row)
        for source in range(count)
        for row in range(2)
    ]
    return lax.ppermute(value, ("st", "row"), pairs)


def swap(value):
    return lax.ppermute(value, "row", [(0, 1), (1, 0)])


def dot(a, b):
    return jnp.dot(a, b, preferred_element_type=jnp.float32)


def scale_kernel(where_ref, own_cols, other_cols, own, other, out):
    del where_ref
    total = dot(own_cols[...], own[...]) + dot(other_cols[...], other[...])
    out[...] = total.astype(out.dtype)


def scale(where, inverse, own, own_spec, other):
    stations, _, rows, wide = inverse.shape
    columns = other.shape[-1]
    half = wide // 2
    return pl.pallas_call(
        scale_kernel,
        out_shape=jax.ShapeDtypeStruct((stations, rows, columns), jnp.bfloat16),
        grid_spec=pltpu.PrefetchScalarGridSpec(
            num_scalar_prefetch=1,
            grid=(stations,),
            in_specs=[
                pl.BlockSpec((None, None, rows, half), lambda j, w: (j, 0, 0, w[0])),
                pl.BlockSpec((None, None, rows, half), lambda j, w: (j, 0, 0, 1 - w[0])),
                own_spec,
                pl.BlockSpec((None, rows, columns), lambda j, w: (j, 0, 0)),
            ],
            out_specs=pl.BlockSpec((None, rows, columns), lambda j, w: (j, 0, 0)),
        ),
        compiler_params=pltpu.CompilerParams(vmem_limit_bytes=16 * 2**20),
        cost_estimate=pl.CostEstimate(
            flops=2 * stations * rows * wide * columns,
            bytes_accessed=2 * stations * rows * (wide + 3 * columns),
            transcendentals=0,
        ),
        name="scale",
    )(where, inverse, inverse, own, other)


def couple_kernel(where_ref, lo_a, lo_b, up_a, up_b, below_a, below_b, above_a, above_b, now, *rest):
    out = rest[-1]
    j = pl.program_id(0)
    below = dot(lo_a[...], below_a[...]) + dot(lo_b[...], below_b[...])
    above = dot(up_a[...], above_a[...]) + dot(up_b[...], above_b[...])
    has_below = (j > 0) | (where_ref[1] == 0)
    has_above = (j < pl.num_programs(0) - 1) | (where_ref[2] == 0)
    coupled = jnp.where(has_below, below, 0.0) + jnp.where(has_above, above, 0.0)
    out[...] = (now[...].astype(jnp.float32) - coupled).astype(out.dtype)


def couple(where, lower, upper, below, above, now, now_spec, out_shape, out_spec, into=None):
    stations, _, rows, wide = lower.shape
    columns = below[0].shape[-1]
    half = wide // 2
    last = stations - 1

    def block(own):
        if own:
            return pl.BlockSpec((None, None, rows, half), lambda j, w: (j, 0, 0, w[0]))
        return pl.BlockSpec((None, None, rows, half), lambda j, w: (j, 0, 0, 1 - w[0]))

    def from_below():
        return pl.BlockSpec((None, rows, columns), lambda j, w: (jnp.maximum(j - w[1], 0), 0, 0))

    def from_above():
        return pl.BlockSpec((None, rows, columns), lambda j, w: (jnp.minimum(j + w[2], last), 0, 0))

    operands = [where, lower, lower, upper, upper, *below, *above, now]
    in_specs = [block(True), block(False), block(True), block(False)]
    in_specs += [from_below(), from_below(), from_above(), from_above(), now_spec]
    aliases = {}
    if into is not None:
        aliases = {len(operands): 0}
        operands.append(into)
        in_specs.append(pl.BlockSpec(memory_space=pl.ANY))
    return pl.pallas_call(
        couple_kernel,
        out_shape=out_shape,
        grid_spec=pltpu.PrefetchScalarGridSpec(
            num_scalar_prefetch=1, grid=(stations,), in_specs=in_specs, out_specs=out_spec
        ),
        input_output_aliases=aliases,
        compiler_params=pltpu.CompilerParams(vmem_limit_bytes=24 * 2**20),
        cost_estimate=pl.CostEstimate(
            flops=4 * stations * rows * wide * columns,
            bytes_accessed=2 * stations * rows * (2 * wide + 6 * columns),
            transcendentals=0,
        ),
        name="couple",
    )(*operands)


def on_device(forcing, inv1, low1, up1, inv2, low2, up2):
    stations, _, rows, columns = forcing.shape
    piece = columns // CHUNKS
    row = lax.axis_index("row")
    position = lax.axis_index("st")
    count = lax.axis_size("st")

    def where(stride):
        wraps = [position < stride, position >= count - stride]
        return jnp.stack([row] + [flag.astype(jnp.int32) for flag in wraps])

    where1, where2 = where(1), where(2)

    def wide_spec(c):
        return pl.BlockSpec((None, None, rows, piece), lambda j, w: (j, 0, 0, c))

    def slim_spec():
        return pl.BlockSpec((None, rows, piece), lambda j, w: (j, 0, 0))

    slim = jax.ShapeDtypeStruct((stations, rows, piece), jnp.bfloat16)

    def neighbours(scaled, stride):
        below_other, above_other = shift_across(scaled, stride), shift_across(scaled, -stride)
        below_own, above_own = shift(scaled, stride), shift(scaled, -stride)
        return (below_own, below_other), (above_own, above_other)

    out = None
    for c in range(CHUNKS):
        mine = forcing[:, 0, :, c * piece : (c + 1) * piece]
        scaled = scale(where1, inv1, forcing, wide_spec(c), swap(mine))
        below, above = neighbours(scaled, 1)
        first = couple(
            where1, low1, up1, below, above, forcing, wide_spec(c), slim, slim_spec()
        )
        scaled = scale(where2, inv2, first, slim_spec(), swap(first))
        below, above = neighbours(scaled, 2)
        out = couple(
            where2, low2, up2, below, above, first, slim_spec(),
            jax.ShapeDtypeStruct(forcing.shape, forcing.dtype), wide_spec(c), out,
        )
    return out


def solution(mesh):
    spec = P(None, "st", "row", None)
    return jax.shard_map(
        on_device, mesh=mesh, in_specs=(spec,) * 7, out_specs=spec, check_vma=False
    )
```

```python
import jax
import jax.numpy as jnp
from jax import lax
from jax.experimental import pallas as pl
from jax.experimental.pallas import tpu as pltpu
from jax.sharding import PartitionSpec as P

FIRST_PIECES, MID_PIECES, LAST_PIECES = 2, 2, 2


def shift(value, steps):
    count = lax.axis_size("st")
    pairs = [(source, (source + steps) % count) for source in range(count)]
    return lax.ppermute(value, "st", pairs)


def shift_across(value, steps):
    count = lax.axis_size("st")
    pairs = [
        (2 * source + row, 2 * ((source + steps) % count) + 1 - row)
        for source in range(count)
        for row in range(2)
    ]
    return lax.ppermute(value, ("st", "row"), pairs)


def swap(value):
    return lax.ppermute(value, "row", [(0, 1), (1, 0)])


def dot(a, b):
    return jnp.dot(a, b, preferred_element_type=jnp.float32)


def half_of(block, j, which):
    half = block.shape[-1] // 2
    return block[j, 0, :, pl.ds(pl.multiple_of(which * half, half), half)]


def side_by_side(refs, j):
    values = [ref[j] for ref in refs]
    return values[0] if len(values) == 1 else jnp.concatenate(values, axis=-1)


def call(kernel, where, operands, outs, flops):
    moved = sum(o.size * o.dtype.itemsize for o in operands) + sum(
        o.size * o.dtype.itemsize for o in outs
    )
    return pl.pallas_call(
        kernel,
        out_shape=outs,
        in_specs=[pl.BlockSpec(memory_space=pltpu.SMEM)]
        + [pl.BlockSpec(memory_space=pltpu.VMEM)] * len(operands),
        out_specs=[pl.BlockSpec(memory_space=pltpu.VMEM)] * len(outs),
        compiler_params=pltpu.CompilerParams(vmem_limit_bytes=32 * 2**20),
        cost_estimate=pl.CostEstimate(flops=flops, bytes_accessed=moved, transcendentals=0),
    )(where, *operands)


def scale_own_kernel(where, inverse, *refs):
    own, out = refs[:-1], refs[-1]
    for j in range(inverse.shape[0]):
        out[j] = dot(half_of(inverse, j, where[0]), side_by_side(own, j))


def scale_other_kernel(count, where, inverse, part, *refs):
    other, outs = refs[:count], refs[count:]
    for j in range(inverse.shape[0]):
        total = part[j] + dot(half_of(inverse, j, 1 - where[0]), side_by_side(other, j))
        total = total.astype(jnp.bfloat16)
        width = outs[0].shape[-1]
        for c, out in enumerate(outs):
            out[j] = total[:, c * width : (c + 1) * width]


def scale(where, inverse, own, other, pieces):
    stations, _, rows, wide = inverse.shape
    columns = sum(o.shape[-1] for o in own)
    flops = stations * rows * wide * columns
    part = call(
        scale_own_kernel, where, [inverse, *own],
        [jax.ShapeDtypeStruct((stations, rows, columns), jnp.float32)], flops,
    )[0]
    outs = [jax.ShapeDtypeStruct((stations, rows, columns // pieces), jnp.bfloat16)] * pieces
    return call(
        lambda *refs: scale_other_kernel(len(other), *refs), where,
        [inverse, part, *other], outs, flops,
    )


def couple_both(where, lower, upper, below, above, j, stations, which):
    below_at = jnp.maximum(j - where[1], 0)
    above_at = jnp.minimum(j + where[2], stations - 1)
    low = dot(half_of(lower, j, which), below[below_at])
    high = dot(half_of(upper, j, which), above[above_at])
    if j == 0:
        low = jnp.where(where[1] == 0, low, 0.0)
    if j == stations - 1:
        high = jnp.where(where[2] == 0, high, 0.0)
    return low + high


def couple_own_kernel(start, where, lower, upper, below, above, now, out):
    stations = lower.shape[0]
    width = out.shape[-1]
    for j in range(stations):
        coupled = couple_both(where, lower, upper, below, above, j, stations, where[0])
        out[j] = now[j][:, start : start + width].astype(jnp.float32) - coupled


def couple_other_kernel(where, lower, upper, below, above, part, *outs):
    stations = lower.shape[0]
    width = outs[0].shape[-1]
    for j in range(stations):
        coupled = couple_both(where, lower, upper, below, above, j, stations, 1 - where[0])
        total = (part[j] - coupled).astype(outs[0].dtype)
        for c, out in enumerate(outs):
            out[j] = total[:, c * width : (c + 1) * width]


def couple_last_kernel(where, lower, upper, below, above, part, *rest):
    out = rest[-1]
    stations = lower.shape[0]
    for j in range(stations):
        @pl.when(pl.program_id(0) == j)
        def _():
            coupled = couple_both(where, lower, upper, below, above, j, stations, 1 - where[0])
            out[...] = (part[j] - coupled).astype(out.dtype)


def on_device(forcing, inv1, low1, up1, inv2, low2, up2):
    stations, _, rows, columns = forcing.shape
    wide = inv1.shape[-1]
    piece = columns // LAST_PIECES
    middle = columns // MID_PIECES
    row = lax.axis_index("row")
    position = lax.axis_index("st")
    count = lax.axis_size("st")

    def where_for(stride):
        wraps = [position < stride, position >= count - stride]
        return jnp.stack([row] + [flag.astype(jnp.int32) for flag in wraps])

    where1, where2 = where_for(1), where_for(2)

    def array(width, dtype=jnp.bfloat16):
        return jax.ShapeDtypeStruct((stations, rows, width), dtype)

    def flops(width):
        return 2 * stations * rows * wide * width

    def spread(scaled, stride):
        def send(move, steps):
            return move(scaled, steps)

        across = send(shift_across, stride), send(shift_across, -stride)
        straight = send(shift, stride), send(shift, -stride)
        return straight, across

    def own_part(where, lower, upper, straight, now, start):
        width = straight[0].shape[-1]
        return call(
            lambda *refs: couple_own_kernel(start, *refs), where,
            [lower, upper, *straight, now], [array(width, jnp.float32)], flops(width),
        )[0]

    flat = forcing.reshape(stations, rows, columns)
    if FIRST_PIECES == 1:
        scaled1 = scale(where1, inv1, [flat], [swap(flat)], MID_PIECES)
    else:
        scaled1 = []
        for c in range(MID_PIECES):
            mine = flat[:, :, c * middle : (c + 1) * middle]
            scaled1 += scale(where1, inv1, [mine], [swap(mine)], 1)
    firsts = []
    for c in range(MID_PIECES):
        straight, across = spread(scaled1[c], 1)
        part = own_part(where1, low1, up1, straight, flat, c * middle)
        firsts += call(
            couple_other_kernel, where1, [low1, up1, *across, part],
            [array(piece)] * (LAST_PIECES // MID_PIECES), flops(middle),
        )
    out = None
    for c in range(LAST_PIECES):
        first = firsts[c]
        other = swap(first)
        (scaled2,) = scale(where2, inv2, [first], [other], 1)
        straight, across = spread(scaled2, 2)
        part = own_part(where2, low2, up2, straight, first, 0)
        operands = [where2, low2, up2, *across, part]
        specs = [pl.BlockSpec(memory_space=pltpu.SMEM)]
        specs += [pl.BlockSpec(memory_space=pltpu.VMEM)] * 5
        aliases = {}
        if out is not None:
            aliases = {len(operands): 0}
            operands.append(out)
            specs.append(pl.BlockSpec(memory_space=pl.ANY))
        run = pl.pallas_call(
            couple_last_kernel,
            grid=(stations,),
            out_shape=jax.ShapeDtypeStruct(forcing.shape, forcing.dtype),
            in_specs=specs,
            out_specs=pl.BlockSpec((None, None, rows, piece), lambda j, c=c: (j, 0, 0, c)),
            input_output_aliases=aliases,
            compiler_params=pltpu.CompilerParams(vmem_limit_bytes=32 * 2**20),
            cost_estimate=pl.CostEstimate(
                flops=flops(piece), bytes_accessed=4 * stations * rows * wide, transcendentals=0
            ),
            name="couple_last",
        )
        out = run(*operands)
    return out


def solution(mesh):
    spec = P(None, "st", "row", None)

    return jax.shard_map(
        on_device, mesh=mesh, in_specs=(spec,) * 7, out_specs=spec, check_vma=False
    )
```

```python
import jax
import jax.numpy as jnp
from jax import lax
from jax.experimental import pallas as pl
from jax.experimental.pallas import tpu as pltpu
from jax.sharding import PartitionSpec as P

FIRST_PIECES, MID_PIECES, LAST_PIECES = 2, 2, 2


def shift(value, steps):
    count = lax.axis_size("st")
    pairs = [(source, (source + steps) % count) for source in range(count)]
    return lax.ppermute(value, "st", pairs)


def shift_across(value, steps):
    count = lax.axis_size("st")
    pairs = [
        (2 * source + row, 2 * ((source + steps) % count) + 1 - row)
        for source in range(count)
        for row in range(2)
    ]
    return lax.ppermute(value, ("st", "row"), pairs)


def swap(value):
    return lax.ppermute(value, "row", [(0, 1), (1, 0)])


def dot(a, b):
    return jnp.dot(a, b, preferred_element_type=jnp.float32)


def half_of(block, j, which):
    half = block.shape[-1] // 2
    return block[j, 0, :, pl.ds(pl.multiple_of(which * half, half), half)]


def side_by_side(refs, j):
    values = [ref[j] for ref in refs]
    return values[0] if len(values) == 1 else jnp.concatenate(values, axis=-1)


def call(kernel, where, operands, outs, flops):
    moved = sum(o.size * o.dtype.itemsize for o in operands) + sum(
        o.size * o.dtype.itemsize for o in outs
    )
    return pl.pallas_call(
        kernel,
        out_shape=outs,
        in_specs=[pl.BlockSpec(memory_space=pltpu.SMEM)]
        + [pl.BlockSpec(memory_space=pltpu.VMEM)] * len(operands),
        out_specs=[pl.BlockSpec(memory_space=pltpu.VMEM)] * len(outs),
        compiler_params=pltpu.CompilerParams(vmem_limit_bytes=32 * 2**20),
        cost_estimate=pl.CostEstimate(flops=flops, bytes_accessed=moved, transcendentals=0),
    )(where, *operands)


def scale_own_kernel(where, inverse, *refs):
    own, out = refs[:-1], refs[-1]
    for j in range(inverse.shape[0]):
        out[j] = dot(half_of(inverse, j, where[0]), side_by_side(own, j))


def scale_other_kernel(count, where, inverse, part, *refs):
    other, outs = refs[:count], refs[count:]
    for j in range(inverse.shape[0]):
        total = part[j] + dot(half_of(inverse, j, 1 - where[0]), side_by_side(other, j))
        total = total.astype(jnp.bfloat16)
        width = outs[0].shape[-1]
        for c, out in enumerate(outs):
            out[j] = total[:, c * width : (c + 1) * width]


def scale(where, inverse, own, other, pieces):
    stations, _, rows, wide = inverse.shape
    columns = sum(o.shape[-1] for o in own)
    flops = stations * rows * wide * columns
    part = call(
        scale_own_kernel, where, [inverse, *own],
        [jax.ShapeDtypeStruct((stations, rows, columns), jnp.float32)], flops,
    )[0]
    outs = [jax.ShapeDtypeStruct((stations, rows, columns // pieces), jnp.bfloat16)] * pieces
    return call(
        lambda *refs: scale_other_kernel(len(other), *refs), where,
        [inverse, part, *other], outs, flops,
    )


def coupled_from(above, where, block, straight, across, j):
    stations = block.shape[0]
    if above:
        index, edge, wraps = jnp.minimum(j + where[2], stations - 1), stations - 1, where[2]
    else:
        index, edge, wraps = jnp.maximum(j - where[1], 0), 0, where[1]
    total = dot(half_of(block, j, where[0]), straight[index])
    total += dot(half_of(block, j, 1 - where[0]), across[index])
    return jnp.where(wraps == 0, total, 0.0) if j == edge else total


def couple_first_kernel(above, start, where, block, straight, across, now, out):
    width = out.shape[-1]
    for j in range(block.shape[0]):
        coupled = coupled_from(above, where, block, straight, across, j)
        out[j] = now[j][:, start : start + width].astype(jnp.float32) - coupled


def couple_second_kernel(above, where, block, straight, across, part, *outs):
    width = outs[0].shape[-1]
    for j in range(block.shape[0]):
        coupled = coupled_from(above, where, block, straight, across, j)
        total = (part[j] - coupled).astype(outs[0].dtype)
        for c, out in enumerate(outs):
            out[j] = total[:, c * width : (c + 1) * width]


def couple_last_kernel(above, where, block, straight, across, part, *rest):
    out = rest[-1]
    for j in range(block.shape[0]):
        @pl.when(pl.program_id(0) == j)
        def _():
            coupled = coupled_from(above, where, block, straight, across, j)
            out[...] = (part[j] - coupled).astype(out.dtype)


def on_device(forcing, inv1, low1, up1, inv2, low2, up2):
    stations, _, rows, columns = forcing.shape
    wide = inv1.shape[-1]
    piece = columns // LAST_PIECES
    middle = columns // MID_PIECES
    row = lax.axis_index("row")
    position = lax.axis_index("st")
    count = lax.axis_size("st")

    def where_for(stride):
        wraps = [position < stride, position >= count - stride]
        return jnp.stack([row] + [flag.astype(jnp.int32) for flag in wraps])

    where1, where2 = where_for(1), where_for(2)

    def array(width, dtype=jnp.bfloat16):
        return jax.ShapeDtypeStruct((stations, rows, width), dtype)

    def flops(width):
        return 2 * stations * rows * wide * width

    def spread(scaled, stride):
        def send(move, steps):
            return move(scaled, steps)

        below = send(shift, stride), send(shift_across, stride)
        above = send(shift, -stride), send(shift_across, -stride)
        return below, above

    def first_part(above, where, block, pieces, now, start):
        width = pieces[0].shape[-1]
        return call(
            lambda *refs: couple_first_kernel(above, start, *refs), where,
            [block, *pieces, now], [array(width, jnp.float32)], flops(width),
        )[0]

    flat = forcing.reshape(stations, rows, columns)
    if FIRST_PIECES == 1:
        scaled1 = scale(where1, inv1, [flat], [swap(flat)], MID_PIECES)
    else:
        scaled1 = []
        for c in range(MID_PIECES):
            source = flat if c == 0 else lax.optimization_barrier((flat, mine))[0]
            mine = source[:, :, c * middle : (c + 1) * middle]
            scaled1 += scale(where1, inv1, [mine], [swap(mine)], 1)
    firsts = []
    for c in range(MID_PIECES):
        below, above = spread(scaled1[c], 1)
        part = first_part(True, where1, up1, above, flat, c * middle)
        firsts += call(
            lambda *refs: couple_second_kernel(False, *refs), where1,
            [low1, *below, part],
            [array(piece)] * (LAST_PIECES // MID_PIECES), flops(middle),
        )
    out = None
    for c in range(LAST_PIECES):
        first = firsts[c]
        other = swap(first)
        (scaled2,) = scale(where2, inv2, [first], [other], 1)
        below, above = spread(scaled2, 2)
        part = first_part(False, where2, low2, below, first, 0)
        operands = [where2, up2, *above, part]
        specs = [pl.BlockSpec(memory_space=pltpu.SMEM)]
        specs += [pl.BlockSpec(memory_space=pltpu.VMEM)] * 4
        aliases = {}
        if out is not None:
            aliases = {len(operands): 0}
            operands.append(out)
            specs.append(pl.BlockSpec(memory_space=pl.ANY))
        run = pl.pallas_call(
            lambda *refs: couple_last_kernel(True, *refs),
            grid=(stations,),
            out_shape=jax.ShapeDtypeStruct(forcing.shape, forcing.dtype),
            in_specs=specs,
            out_specs=pl.BlockSpec((None, None, rows, piece), lambda j, c=c: (j, 0, 0, c)),
            input_output_aliases=aliases,
            compiler_params=pltpu.CompilerParams(vmem_limit_bytes=32 * 2**20),
            cost_estimate=pl.CostEstimate(
                flops=flops(piece), bytes_accessed=2 * stations * rows * wide, transcendentals=0
            ),
            name="couple_last",
        )
        out = run(*operands)
    return out


def solution(mesh):
    spec = P(None, "st", "row", None)

    return jax.shard_map(
        on_device, mesh=mesh, in_specs=(spec,) * 7, out_specs=spec, check_vma=False
    )
```
